32 devices in a mesh: groups: 2 (over x), sect: 8 (over z, y), head: 2 (over core).
Axes of the slice: x: 2, y: 2, z: 4, core: 2. Of those that a mesh axis runs over, the one named last changes fastest.
Arguments:
- queries: bfloat16 [2048, 8192], P(('groups', 'sect'), 'head'), parts along dimension 0, may hold values from -200 to 200
- packed_key_rows: bfloat16 [2048, 512], P(('groups', 'sect'), 'head'), parts along dimension 0, may hold values from -7 to 7
- values: bfloat16 [2048, 512], P(('groups', 'sect'), 'head'), parts along dimension 0, may hold values from -12 to 12
- segments: int32 [2048], P('groups'), parts along dimension 0, may hold values from 0 to 7, never falling along the last dimension, each value on 1 to 512 neighbouring positions
- proj_weight: bfloat16 [8192, 2048], P('head', 'sect'), may hold values from -0.0625 to 0.0625
- residual: bfloat16 [2048, 2048], P(('groups', 'sect', 'head')), parts along dimension 0, may hold values from -2 to 2
- norm_gain: bfloat16 [2048], replicated, may hold values from 0.5 to 1.5
- expert_ids: int32 [2048, 8], P(('groups', 'sect', 'head')), parts along dimension 0, may hold values from 0 to 15, all different within a row; in each aligned block of 64 rows (0 to 63, 64 to 127, ...) at most 48 rows name the same one
- route_weights: float32 [2048, 8], P(('groups', 'sect', 'head')), parts along dimension 0, may hold values from 0.05 to 1
- gate_weight: bfloat16 [16, 2048, 768], P(('sect', 'head')), may hold values from -0.125 to 0.125
- up_weight: bfloat16 [16, 2048, 768], P(('sect', 'head')), may hold values from -0.125 to 0.125
- down_weight: bfloat16 [16, 768, 2048], P(('sect', 'head')), may hold values from -0.21875 to 0.21875
Outputs:
- hidden_mid: bfloat16 [2048, 2048], P(('groups', 'sect', 'head')), parts along dimension 0
- expert_mix: bfloat16 [2048, 2048], P(('groups', 'sect', 'head')), parts along dimension 0
The draws below stay inside these ranges and needn't reach their ends.
There are 2 independent parts, one for each index of `groups`. The reference program is written for one: setup_inputs(seed, part) draws one part's arguments, and reference() takes and returns one part's arrays. A program takes and returns all parts, laid end to end along the dimension named above; an argument that names none is the same for every part. Nothing has to cross between parts.
Inputs may be any that keep to these rules, and one draw needn't show every extreme that they name: `segments`: ids never fall along the rows; each of the 8 prompts has 1 to 512 rows, and one has exactly that many. `expert_ids`: each row names 8 different experts. Within the rows of one device (aligned blocks of 64 rows) no expert is named by more than 48 rows.
All inputs are finite; a program needn't handle non-finite values.
Results may differ from the reference program's by a relative error of at most 0.02.
Values may be sent and summed in bfloat16 or wider, within the bound.
A program may use at most 256 MiB of HBM per device.

```python
import math
import jax
import jax.numpy as jnp
import numpy as np
from jax import lax

D = 2048
FF = 768
QUERY_HEADS = 64
KEY_VALUE_HEADS = 4
HEAD_WIDTH = 128
TOPK = 8
PROMPTS = 8
SECTION_ROWS = 128
TOKEN_TOTAL = 1024
MOE_ROWS = 64
EXPERTS = 16
CAP = 48
N_SECT = 8
N_HEAD = 2


def base_keys(key):
    unshaped_draw = jax.random.normal(jax.random.fold_in(key, 11), (TOKEN_TOTAL, KEY_VALUE_HEADS, HEAD_WIDTH), jnp.float32)
    return jnp.clip(unshaped_draw, -6.0, 6.0)


def draw_packed_key_rows(key, part):
    key_random_draw = base_keys(key)
    return key_random_draw.reshape(TOKEN_TOTAL, KEY_VALUE_HEADS * HEAD_WIDTH).astype(jnp.bfloat16)


def draw_queries(key, part):
    query_draw = jnp.clip(jax.random.normal(jax.random.fold_in(key, 12), (TOKEN_TOTAL, QUERY_HEADS, HEAD_WIDTH), jnp.float32), -6.0, 6.0)
    return query_draw.reshape(TOKEN_TOTAL, QUERY_HEADS * HEAD_WIDTH).astype(jnp.bfloat16)


def steps_of(key, extent, split, low, top_value):
    factor_of = 1.0
    for position, parts in split:
        draws = jax.random.uniform(jax.random.fold_in(jax.random.fold_in(key, 6), position), (parts,), jnp.float32, low / len(split), top_value / len(split))
        factor_of = factor_of * jnp.repeat(jnp.exp(draws), extent[position] // parts).reshape((-1,) + (1,) * (len(extent) - 1 - position))
    return factor_of


def length_profile(number_of, total, most, slope):
    loads = [(1 << 20) // math.isqrt(standing ** slope) + 1 for standing in range(2, number_of + 1)]
    rest, given = total - most - (number_of - 1), [1] * (number_of - 1)
    while rest > 0:
        movable = [i for i in range(number_of - 1) if given[i] < most]
        whole, budget = sum([loads[i] for i in movable]), rest
        for i in movable:
            addition = min(most - given[i], max(1, budget * loads[i] // whole), rest)
            given[i] = given[i] + addition
            rest = rest - addition
    return np.array([most] + given)


def ragged_sizes(own_key, count, total, most, slope):
    if count == 2:
        one = jax.random.randint(own_key, (), max(1, total - most), min(most, total - 1) + 1)
        return jnp.stack([one, total - one])
    sizes = jnp.asarray(length_profile(count, total, most, slope), jnp.int32)
    pairs = (count - 1) // 2
    giver, receiver = sizes[1:1 + 2 * pairs:2], sizes[2:2 + 2 * pairs:2]
    slack = jnp.minimum(giver - 1, most - receiver)
    shifted = jax.random.randint(jax.random.fold_in(own_key, 1), (pairs,), 0, 1 << 20) % (slack + 1)
    sizes = sizes.at[1:1 + 2 * pairs:2].set(giver - shifted).at[2:2 + 2 * pairs:2].set(receiver + shifted)
    return sizes[jax.random.permutation(jax.random.fold_in(own_key, 2), count)]


def deal_out(key, own, number, rows, count, top, most, skew):
    order = jax.random.permutation(key, count)
    heavy_load, usual = portions_of(count, rows * top, most, skew, True), portions_of(count, rows * top, most, skew, False)
    places = jnp.arange(count)

    def named(sizes, turn):
        used = int((sizes > 0).sum())
        fixed = max(1, used // 4)
        moved = fixed + (places - fixed + turn * (used - fixed)) % max(1, count - fixed)
        return jnp.zeros((count,), jnp.int32).at[order[jnp.where(places < fixed, places, moved)]].set(jnp.asarray(sizes, jnp.int32))

    sizes = jnp.where(number % 4 == 0, named(heavy_load, number // 4), named(usual, number - number // 4 - 1))
    mixed = jax.random.permutation(jax.random.fold_in(own, 3), count)
    donor, receiver = mixed[0:count // 2 * 2:2], mixed[1:count // 2 * 2:2]
    slack = jnp.minimum(sizes[donor] - 1, most - sizes[receiver]) // 2
    slack = jnp.where((donor == order[0]) | (receiver == order[0]) | (sizes[receiver] == 0), 0, jnp.maximum(slack, 0))
    moved = jax.random.randint(jax.random.fold_in(own, 4), (count // 2,), 0, 1 << 20) % (slack + 1)
    sizes = sizes.at[donor].add(-moved).at[receiver].add(moved)
    items = jnp.searchsorted(jnp.cumsum(sizes), jnp.arange(rows * top), side="right").astype(jnp.int32)
    table = items.reshape(top, rows).T
    table = table[jax.random.permutation(jax.random.fold_in(own, 1), rows)]
    turn = jax.random.randint(jax.random.fold_in(own, 2), (rows, 1), 0, top)
    return jnp.take_along_axis(table, (jnp.arange(top)[None, :] + turn) % top, axis=1)


def portions_of(number_of, total, bound, skew, full):
    weights = [(1 << 20) // math.isqrt(rank ** skew) + 1 for rank in range(1, number_of + 1)]
    largest = bound if full else min(bound, max(-(-total // number_of), total * weights[0] // sum(weights)))
    least = 1 if total - largest >= number_of - 1 else 0
    counts, surplus = [largest] + [least] * (number_of - 1), total - largest - least * (number_of - 1)
    while surplus > 0:
        candidates = [i for i in range(1, number_of) if counts[i] < largest] or [i for i in range(1, number_of) if counts[i] < bound]
        mass, remaining = sum([weights[i] for i in candidates]), surplus
        for i in candidates:
            extra = min(bound - counts[i], max(1, remaining * weights[i] // mass), surplus)
            counts[i] = counts[i] + extra
            surplus = surplus - extra
    return np.array(counts)


def scatter_about(key, shape, width, reach, split=(), kind=jnp.bfloat16):
    entries = width * jax.random.normal(key, shape, jnp.float32)
    if split:
        entries = entries * steps_of(key, shape, split, -0.22, 0.18)
    return jnp.clip(entries, -reach, reach).astype(kind)


def setup_inputs(seed: int = 0, part: int = 0) -> dict:
    keys = jax.random.split(jax.random.key(seed), 13)
    part_splits = jax.random.split(jax.random.fold_in(keys[12], part), 13)
    queries = draw_queries(jax.random.fold_in(jax.random.fold_in(keys[12], part), 71), part)
    packed_key_rows = draw_packed_key_rows(jax.random.fold_in(jax.random.fold_in(keys[12], part), 71), part)
    values = scatter_about(part_splits[2], (TOKEN_TOTAL, KEY_VALUE_HEADS * HEAD_WIDTH), 2.0, 12.0, ((0, 8), (1, 2)))
    segments = jnp.searchsorted(jnp.cumsum(ragged_sizes(part_splits[3], PROMPTS, TOKEN_TOTAL, TOKEN_TOTAL // 2, 2)), jnp.arange(TOKEN_TOTAL), side="right").astype(jnp.int32)
    proj_weight = scatter_about(keys[4], (QUERY_HEADS * HEAD_WIDTH, D), (QUERY_HEADS * HEAD_WIDTH) ** -0.5, 0.0625, ((0, 2), (1, 8)))
    residual = scatter_about(part_splits[5], (TOKEN_TOTAL, D), 0.25, 2.0, ((0, 16),))
    norm_gain = jnp.clip(1.0 + 0.1 * jax.random.normal(keys[6], (D,), jnp.float32), 0.5, 1.5).astype(jnp.bfloat16)
    expert_ids_keys = jax.random.split(jax.random.fold_in(part_splits[7], 1), TOKEN_TOTAL // MOE_ROWS)
    expert_ids_turns = jax.random.permutation(jax.random.fold_in(part_splits[7], 3), TOKEN_TOTAL // MOE_ROWS)
    expert_ids = jax.vmap(lambda own, number: deal_out(jax.random.fold_in(part_splits[7], 2), own, number, MOE_ROWS, EXPERTS, TOPK, CAP, 2))(expert_ids_keys, expert_ids_turns).reshape((TOKEN_TOTAL, TOPK))
    route_weights = jnp.clip(jnp.exp(math.log(1.0) - 2.9957323 * jax.random.uniform(part_splits[8], (TOKEN_TOTAL, TOPK), jnp.float32) ** steps_of(part_splits[8], (TOKEN_TOTAL, TOPK), ((0, 16),), -0.2, 0.2)), 0.05, 1.0)
    gate_weight = scatter_about(keys[9], (EXPERTS, D, FF), D ** -0.5, 0.125, ((0, 16),))
    up_weight = scatter_about(keys[10], (EXPERTS, D, FF), D ** -0.5, 0.125, ((0, 16),))
    down_weight = scatter_about(keys[11], (EXPERTS, FF, D), FF ** -0.5, 0.21875, ((0, 16),))
    return {"queries": queries, "packed_key_rows": packed_key_rows, "values": values, "segments": segments, "proj_weight": proj_weight, "residual": residual, "norm_gain": norm_gain, "expert_ids": expert_ids, "route_weights": route_weights, "gate_weight": gate_weight, "up_weight": up_weight, "down_weight": down_weight}


negative_large = -1e+30
norm_eps = 1e-06

def attention_block(block_pos, queries, packed_key_rows, values, segments):
    query_group_width = QUERY_HEADS // KEY_VALUE_HEADS
    key_window_length = min(128, TOKEN_TOTAL)
    key_block_count = TOKEN_TOTAL // key_window_length
    beginning_row = (block_pos * SECTION_ROWS).astype(jnp.int32)
    query_tensor_four = lax.dynamic_slice_in_dim(queries, beginning_row, SECTION_ROWS, 0).astype(jnp.float32).reshape(SECTION_ROWS, KEY_VALUE_HEADS, query_group_width, HEAD_WIDTH)
    query_pos = beginning_row + jnp.arange(SECTION_ROWS, dtype=jnp.int32)
    query_seg = lax.dynamic_slice_in_dim(segments, beginning_row, SECTION_ROWS, 0)
    seg_start = lax.optimization_barrier(jnp.sum((segments[None, :] < query_seg[:, None]).astype(jnp.int32), axis=1))
    lowest = jnp.min(seg_start)
    highest = jnp.max(query_pos)
    score_scale = 1.0 / math.sqrt(HEAD_WIDTH)

    def piece_scores(block_index):
        key_begin_index = (block_index * key_window_length).astype(jnp.int32)
        key_tensor_three = lax.dynamic_slice_in_dim(packed_key_rows, key_begin_index, key_window_length, 0).astype(jnp.float32).reshape(key_window_length, KEY_VALUE_HEADS, HEAD_WIDTH)
        scores = jnp.einsum('rkgd,pkd->rkgp', query_tensor_four, key_tensor_three, precision=lax.Precision.HIGHEST) * score_scale
        key_pos = key_begin_index + jnp.arange(key_window_length, dtype=jnp.int32)
        key_seg = lax.dynamic_slice_in_dim(segments, key_begin_index, key_window_length, 0)
        allowed = jnp.logical_and(key_seg[None, :] == query_seg[:, None], key_pos[None, :] <= query_pos[:, None])
        return (scores, allowed[:, None, None, :], key_begin_index)

    def needed(block_index):
        key_begin_index = block_index * key_window_length
        return jnp.logical_and(key_begin_index <= highest, key_begin_index + key_window_length - 1 >= lowest)

    def maximum_update(block_index, run_max):

        def compute(current):
            scores, allowed, key_begin_index = piece_scores(block_index)
            return jnp.maximum(current, lax.optimization_barrier(jnp.max(jnp.where(allowed, scores, negative_large), axis=-1)))
        return lax.cond(needed(block_index), compute, lambda running: running, run_max)
    row_maximum = lax.fori_loop(0, key_block_count, maximum_update, jnp.full((SECTION_ROWS, KEY_VALUE_HEADS, query_group_width), negative_large, jnp.float32))

    def sum_step(block_index, running):

        def compute(current):
            weight_sum, run_acc = current
            scores, allowed, key_begin_index = piece_scores(block_index)
            weights = jnp.where(allowed, jnp.exp(scores - row_maximum[..., None]), 0.0).astype(jnp.bfloat16)
            weights = lax.optimization_barrier(weights).astype(jnp.float32)
            value_tensor_three = lax.dynamic_slice_in_dim(values, key_begin_index, key_window_length, 0).astype(jnp.float32).reshape(key_window_length, KEY_VALUE_HEADS, HEAD_WIDTH)
            run_acc = run_acc + jnp.einsum('rkgp,pkd->rkgd', weights, value_tensor_three, precision=lax.Precision.HIGHEST)
            return (weight_sum + lax.optimization_barrier(jnp.sum(weights, axis=-1)), run_acc)
        return lax.cond(needed(block_index), compute, lambda kept: kept, running)
    initial_state = (jnp.zeros((SECTION_ROWS, KEY_VALUE_HEADS, query_group_width), jnp.float32), jnp.zeros((SECTION_ROWS, KEY_VALUE_HEADS, query_group_width, HEAD_WIDTH), jnp.float32))
    weight_sum, run_acc = lax.fori_loop(0, key_block_count, sum_step, initial_state)
    return (run_acc / weight_sum[..., None]).reshape(SECTION_ROWS, QUERY_HEADS * HEAD_WIDTH).astype(jnp.bfloat16)

def reference(queries, packed_key_rows, values, segments, proj_weight, residual, norm_gain, expert_ids, route_weights, gate_weight, up_weight, down_weight):
    attended = lax.map(lambda block_pos: attention_block(block_pos, queries, packed_key_rows, values, segments), jnp.arange(TOKEN_TOTAL // SECTION_ROWS, dtype=jnp.int32))
    attended = attended.reshape(TOKEN_TOTAL, QUERY_HEADS * HEAD_WIDTH)
    projected = jnp.dot(attended, proj_weight, preferred_element_type=jnp.float32)
    hidden_mid = (residual.astype(jnp.float32) + projected).astype(jnp.bfloat16)
    mid_float = lax.optimization_barrier(hidden_mid).astype(jnp.float32)
    inverse = lax.rsqrt(lax.optimization_barrier(jnp.mean(mid_float * mid_float, axis=1, keepdims=True)) + norm_eps)
    normed = (mid_float * inverse * norm_gain.astype(jnp.float32)[None, :]).astype(jnp.bfloat16)
    route_share = (route_weights / lax.optimization_barrier(jnp.sum(route_weights, axis=1, keepdims=True))).reshape(-1)
    flat_ids = expert_ids.reshape(-1)
    slot_total = N_SECT * N_HEAD * CAP

    def expert_step(mixture, expert):
        named = flat_ids == expert
        picked = jnp.nonzero(named, size=slot_total, fill_value=0)[0].astype(jnp.int32)
        valid_slot = jnp.arange(slot_total, dtype=jnp.int32) < jnp.sum(named.astype(jnp.int32))
        row_ids = picked // TOPK
        inputs = normed[row_ids]
        gate_act = jnp.dot(inputs, gate_weight[expert], preferred_element_type=jnp.float32)
        up_act = jnp.dot(inputs, up_weight[expert], preferred_element_type=jnp.float32)
        hidden = (jax.nn.silu(gate_act) * up_act).astype(jnp.bfloat16)
        result = jnp.dot(hidden, down_weight[expert], preferred_element_type=jnp.float32).astype(jnp.bfloat16)
        result = lax.optimization_barrier(result).astype(jnp.float32)
        weight = jnp.where(valid_slot, route_share[picked], 0.0)
        mixture = mixture.at[row_ids].add(weight[:, None] * result)
        return (mixture, None)
    mixture, unused = lax.scan(expert_step, jnp.zeros((TOKEN_TOTAL, D), jnp.float32), jnp.arange(EXPERTS, dtype=jnp.int32))
    return (hidden_mid, mixture.astype(jnp.bfloat16))
```

```python
import functools
import math

import jax
import jax.numpy as jnp
from jax import lax
from jax.experimental import pallas as pl
from jax.experimental.pallas import tpu as pltpu
from jax.sharding import PartitionSpec as P

HEAD_WIDTH = 128
MASKED = -1e30
NORM_EPS = 1e-06
MESH = pl.DeviceIdType.MESH
VMEM_SPEC = pl.BlockSpec(memory_space=pltpu.VMEM)
ANY_SPEC = pl.BlockSpec(memory_space=pl.ANY)
DMA = pltpu.SemaphoreType.DMA


def greet(devices):
    barrier = pltpu.get_barrier_semaphore()
    for device in devices:
        pl.semaphore_signal(barrier, inc=1, device_id=device, device_id_type=MESH)
    pl.semaphore_wait(barrier, len(devices))


def remote(src, dst, send_sem, recv_sem, device):
    return pltpu.make_async_remote_copy(
        src_ref=src,
        dst_ref=dst,
        send_sem=send_sem,
        recv_sem=recv_sem,
        device_id=device,
        device_id_type=MESH,
    )


def attention_kernel(
    groups,
    sects,
    kv_heads,
    q_ref,
    kv_ref,
    seg_q_ref,
    seg_k_ref,
    w_ref,
    a_out,
    w_out,
    kv_all,
    att,
    bias,
    kz_send,
    kz_recv,
    ky_send,
    ky_recv,
    a_send,
    a_recv,
    w_send,
    w_recv,
    f_send,
    f_recv,
    local_sem,
):
    g = lax.axis_index("groups")
    s = lax.axis_index("sect")
    halves = sects // 2
    h = s // 2
    low = lax.rem(s, 2)
    rows = q_ref.shape[0]
    cols = q_ref.shape[1] // sects
    w_cols = w_ref.shape[1]
    w_rows = w_ref.shape[0] // sects
    part = w_rows // groups
    other_y = 2 * h + 1 - low
    sect_peers = [lax.rem(s + i, sects) for i in range(1, sects)]
    group_peers = [lax.rem(g + i, groups) for i in range(1, groups)]
    greet([{"sect": t} for t in sect_peers] + [{"groups": t} for t in group_peers])
    started = []

    def kv_cross(t):
        return remote(
            kv_ref if t is None else kv_all.at[2 * t + low],
            kv_all.at[s if t is None else 2 * t + low],
            ky_send.at[h if t is None else t],
            ky_recv.at[h if t is None else t],
            {"sect": other_y},
        )

    for i in range(1, halves):
        t = lax.rem(h + i, halves)
        copy = remote(
            kv_ref, kv_all.at[s], kz_send.at[t], kz_recv.at[h], {"sect": 2 * t + low}
        )
        copy.start()
        started.append(copy)
    copy = kv_cross(None)
    copy.start()
    started.append(copy)
    own_kv = pltpu.make_async_copy(kv_ref, kv_all.at[s], local_sem.at[0])
    own_kv.start()

    def w_piece(t):
        return w_ref.at[pl.ds(pl.multiple_of(t * w_rows + g * part, part), part), :]

    def w_place(group, t):
        span = pl.ds(pl.multiple_of(group * part, part), part)
        if len(w_out.shape) == 3:
            return w_out.at[t, span, :]
        return w_out.at[span, pl.ds(pl.multiple_of(t * w_cols, w_cols), w_cols)]

    for t in sect_peers:
        copy = remote(
            w_piece(t), w_place(g, s), w_send.at[t], w_recv.at[s], {"sect": t}
        )
        copy.start()
        started.append(copy)
    own_w = pltpu.make_async_copy(w_piece(s), w_place(g, s), local_sem.at[1])
    own_w.start()
    for i, t in enumerate(group_peers):
        copy = remote(
            w_piece(s), w_place(g, s), f_send.at[i, s], f_recv.at[g, s], {"groups": t}
        )
        copy.start()
        started.append(copy)

    for i in range(1, halves):
        t = lax.rem(h + i, halves)
        remote(
            kv_ref, kv_all.at[2 * t + low], kz_send.at[t], kz_recv.at[t], {"sect": 2 * t + low}
        ).wait_recv()
        copy = kv_cross(t)
        copy.start()
        started.append(copy)

    window = seg_k_ref.shape[1]
    first = jnp.maximum(s - (window // rows - 1), 0)
    q_pos = s * rows + lax.broadcasted_iota(jnp.int32, (rows, window), 0)
    k_pos = first * rows + lax.broadcasted_iota(jnp.int32, (rows, window), 1)
    allowed = jnp.logical_and(seg_q_ref[...] == seg_k_ref[...], k_pos <= q_pos)
    bias[...] = jnp.where(allowed, 0.0, MASKED)

    for i in range(halves):
        t = lax.rem(h + i, halves)
        remote(
            kv_ref, kv_all.at[2 * t + 1 - low], ky_send.at[t], ky_recv.at[t], {"sect": other_y}
        ).wait_recv()
    own_kv.wait()

    scale = 1.0 / math.sqrt(HEAD_WIDTH)
    kv_width = kv_heads * HEAD_WIDTH
    per_kv = q_ref.shape[1] // kv_heads

    def attend(i, carry):
        t = lax.rem(s + 1 + i, sects)
        kv_head = (t * cols) // per_kv
        k_col = pl.multiple_of(kv_head * HEAD_WIDTH, HEAD_WIDTH)
        v_col = pl.multiple_of(kv_width + kv_head * HEAD_WIDTH, HEAD_WIDTH)
        span = pl.ds(first, window // rows)
        keys = kv_all[span, :, pl.ds(k_col, HEAD_WIDTH)].reshape(window, HEAD_WIDTH)
        vals = kv_all[span, :, pl.ds(v_col, HEAD_WIDTH)].reshape(window, HEAD_WIDTH)
        for j in range(cols // HEAD_WIDTH):
            q_col = pl.multiple_of(t * cols + j * HEAD_WIDTH, HEAD_WIDTH)
            q = q_ref[:, pl.ds(q_col, HEAD_WIDTH)]
            scores = lax.dot_general(
                q, keys, (((1,), (1,)), ((), ())), preferred_element_type=jnp.float32
            )
            scores = scores * scale + bias[...]
            top = jnp.max(scores, axis=1, keepdims=True)
            weights = jnp.exp(scores - top).astype(jnp.bfloat16)
            total = jnp.sum(weights.astype(jnp.float32), axis=1, keepdims=True)
            mixed = jnp.dot(weights, vals, preferred_element_type=jnp.float32)
            att[t, :, j * HEAD_WIDTH : (j + 1) * HEAD_WIDTH] = (mixed / total).astype(
                jnp.bfloat16
            )
        return carry

    def a_place(t):
        return a_out.at[pl.ds(pl.multiple_of(t * rows, rows), rows), :]

    def a_copy(t):
        return remote(att.at[t], a_place(s), a_send.at[t], a_recv.at[s], {"sect": t})

    def step(i, carry):
        attend(i, carry)

        @pl.when(i >= 1)
        def _():
            a_copy(lax.rem(s + i, sects)).start()

        return carry

    lax.fori_loop(0, sects, step, 0)
    own_a = pltpu.make_async_copy(att.at[s], a_place(s), local_sem.at[2])
    own_a.start()

    for t in sect_peers:
        remote(
            w_piece(s), w_place(g, t), w_send.at[t], w_recv.at[t], {"sect": t}
        ).wait_recv()
        for i, u in enumerate(group_peers):
            copy = remote(
                w_place(g, t), w_place(g, t), f_send.at[i, t], f_recv.at[g, t], {"groups": u}
            )
            copy.start()
            started.append(copy)
    for t in sect_peers:
        remote(att.at[t], a_place(t), a_send.at[t], a_recv.at[t], {"sect": t}).wait_recv()
    for u in group_peers:
        for t in [s] + sect_peers:
            remote(
                w_place(g, t), w_place(u, t), f_send.at[0, t], f_recv.at[u, t], {"groups": u}
            ).wait_recv()
    own_w.wait()
    own_a.wait()
    for copy in started:
        copy.wait_send()
    for t in sect_peers:
        a_copy(t).wait_send()


def exchange_attention(queries, kv, seg_q, seg_k, proj_weight, kv_heads):
    groups = lax.axis_size("groups")
    sects = lax.axis_size("sect")
    rows, width = queries.shape
    cols = width // sects
    w_rows = proj_weight.shape[0] // sects
    w_cols = proj_weight.shape[1]
    aligned = w_cols % 128 == 0
    w_shape = (w_rows, w_cols * sects) if aligned else (sects, w_rows, w_cols)
    attended, weight = pl.pallas_call(
        functools.partial(attention_kernel, groups, sects, kv_heads),
        out_shape=(
            jax.ShapeDtypeStruct((rows * sects, cols), jnp.bfloat16),
            jax.ShapeDtypeStruct(w_shape, jnp.bfloat16),
        ),
        in_specs=[VMEM_SPEC, VMEM_SPEC, VMEM_SPEC, VMEM_SPEC, ANY_SPEC],
        out_specs=(ANY_SPEC, ANY_SPEC),
        scratch_shapes=[
            pltpu.VMEM((sects,) + kv.shape, jnp.bfloat16),
            pltpu.VMEM((sects, rows, cols), jnp.bfloat16),
            pltpu.VMEM((rows, seg_k.shape[1]), jnp.float32),
            DMA((sects // 2,)),
            DMA((sects // 2,)),
            DMA((sects // 2,)),
            DMA((sects // 2,)),
            DMA((sects,)),
            DMA((sects,)),
            DMA((sects,)),
            DMA((sects,)),
            DMA((groups, sects)),
            DMA((groups, sects)),
            DMA((3,)),
        ],
        compiler_params=pltpu.CompilerParams(collective_id=0, has_side_effects=True),
        name="attention",
    )(queries, kv, seg_q, seg_k, proj_weight)
    if not aligned:
        weight = weight.transpose(1, 0, 2).reshape(w_rows, w_cols * sects)
    return attended, weight


def positions():
    s = lax.axis_index("sect")
    c = lax.axis_index("head")
    halves = lax.axis_size("sect") // 2
    h = s // 2
    low = lax.rem(s, 2)
    partner = {"head": 1 - c}
    across = {"sect": 2 * h + 1 - low}
    others = [lax.rem(h + i, halves) for i in range(1, halves)]
    return s, c, h, low, halves, partner, across, others


def sum_kernel(
    p_ref, o_ref, rp, cs, ry, zs, rz, p_send, p_recv, y_send, y_recv, z_send, z_recv
):
    s, c, h, low, halves, partner, across, others = positions()
    greet([partner, across] + [{"sect": 2 * t + low} for t in others])
    order = others + [h]
    started = []

    def widen(x):
        return x.astype(jnp.float32)

    for t in order:
        copy = remote(
            p_ref.at[pl.ds(2 * t, 2), 1 - c], rp.at[t], p_send.at[t], p_recv.at[t], partner
        )
        copy.start()
        started.append(copy)
    for t in order:
        remote(
            p_ref.at[pl.ds(2 * t, 2), 1 - c], rp.at[t], p_send.at[t], p_recv.at[t], partner
        ).wait_recv()
        cs[t] = (widen(p_ref[2 * t + 1 - low, c]) + widen(rp[t, 1 - low])).astype(jnp.bfloat16)
        copy = remote(cs.at[t], ry.at[t], y_send.at[t], y_recv.at[t], across)
        copy.start()
        started.append(copy)
    for t in order:
        remote(cs.at[t], ry.at[t], y_send.at[t], y_recv.at[t], across).wait_recv()
        total = widen(p_ref[2 * t + low, c]) + widen(rp[t, low]) + widen(ry[t])
        if t is h:
            o_ref[...] = total
        else:
            zs[t] = total.astype(jnp.bfloat16)
            copy = remote(
                zs.at[t], rz.at[h], z_send.at[t], z_recv.at[h], {"sect": 2 * t + low}
            )
            copy.start()
            started.append(copy)
    for t in others:
        remote(
            zs.at[t], rz.at[t], z_send.at[t], z_recv.at[t], {"sect": 2 * t + low}
        ).wait_recv()
        o_ref[...] += widen(rz[t])
    for copy in started:
        copy.wait_send()


def sum_scatter(partial_rows, moe_rows, collective_id):
    sects = lax.axis_size("sect")
    heads = lax.axis_size("head")
    width = partial_rows.shape[1]
    halves = sects // 2
    block = (moe_rows, width)
    return pl.pallas_call(
        sum_kernel,
        out_shape=jax.ShapeDtypeStruct(block, jnp.float32),
        in_specs=[VMEM_SPEC],
        out_specs=VMEM_SPEC,
        scratch_shapes=[
            pltpu.VMEM((halves, 2) + block, jnp.bfloat16),
            pltpu.VMEM((halves,) + block, jnp.bfloat16),
            pltpu.VMEM((halves,) + block, jnp.bfloat16),
            pltpu.VMEM((halves,) + block, jnp.bfloat16),
            pltpu.VMEM((halves,) + block, jnp.bfloat16),
        ]
        + [DMA((halves,))] * 6,
        compiler_params=pltpu.CompilerParams(
            collective_id=collective_id, has_side_effects=True
        ),
        name="sum_scatter",
    )(partial_rows.reshape((sects, heads) + block))


def gather_kernel(
    x_ref, o_ref, p_send, p_recv, y_send, y_recv, z_send, z_recv, local_sem
):
    s, c, h, low, halves, partner, across, others = positions()
    greet([partner, across] + [{"sect": 2 * t + low} for t in others])
    started = []

    def send(src, row, send_sem, recv_sem, device):
        copy = remote(src, o_ref.at[row, c], send_sem, recv_sem, device)
        copy.start()
        started.append(copy)

    for t in others:
        send(x_ref, s, z_send.at[t], z_recv.at[h], {"sect": 2 * t + low})
    send(x_ref, s, y_send.at[h], y_recv.at[h], across)
    send(x_ref, s, p_send.at[s], p_recv.at[s], partner)
    own = pltpu.make_async_copy(x_ref, o_ref.at[s, c], local_sem)
    own.start()
    for t in others:
        row = 2 * t + low
        remote(x_ref, o_ref.at[row, c], z_send.at[t], z_recv.at[t], {"sect": row}).wait_recv()
        send(o_ref.at[row, c], row, y_send.at[t], y_recv.at[t], across)
        send(o_ref.at[row, c], row, p_send.at[row], p_recv.at[row], partner)
    for t in [h] + others:
        row = 2 * t + 1 - low
        remote(x_ref, o_ref.at[row, c], y_send.at[t], y_recv.at[t], across).wait_recv()
        send(o_ref.at[row, c], row, p_send.at[row], p_recv.at[row], partner)
    for t in [h] + others:
        for row in (2 * t + low, 2 * t + 1 - low):
            remote(
                x_ref, o_ref.at[row, 1 - c], p_send.at[row], p_recv.at[row], partner
            ).wait_recv()
    own.wait()
    for copy in started:
        copy.wait_send()


def gather_rows(x, collective_id):
    sects = lax.axis_size("sect")
    heads = lax.axis_size("head")
    halves = sects // 2
    out = pl.pallas_call(
        gather_kernel,
        out_shape=jax.ShapeDtypeStruct((sects, heads) + x.shape, x.dtype),
        in_specs=[VMEM_SPEC],
        out_specs=VMEM_SPEC,
        scratch_shapes=[
            DMA((sects,)),
            DMA((sects,)),
            DMA((halves,)),
            DMA((halves,)),
            DMA((halves,)),
            DMA((halves,)),
            DMA,
        ],
        compiler_params=pltpu.CompilerParams(
            collective_id=collective_id, has_side_effects=True
        ),
        name="gather_rows",
    )(x)
    return out.reshape(-1, x.shape[1])


def shards(
    queries,
    packed_key_rows,
    values,
    segments,
    proj_weight,
    residual,
    norm_gain,
    expert_ids,
    route_weights,
    gate_weight,
    up_weight,
    down_weight,
):
    rows = queries.shape[0]
    sects = lax.axis_size("sect")
    heads = lax.axis_size("head")
    s = lax.axis_index("sect")
    c = lax.axis_index("head")
    experts = sects * heads
    moe_rows, width = residual.shape
    kv_heads = packed_key_rows.shape[1] // HEAD_WIDTH

    blocks = min(sects, -(-segments.shape[0] // (2 * rows)) + 1)
    first = jnp.maximum(s - (blocks - 1), 0)
    seg_q = lax.dynamic_slice_in_dim(segments, s * rows, rows, 0)[:, None]
    seg_k = lax.dynamic_slice_in_dim(segments, first * rows, blocks * rows, 0)[None, :]
    kv = jnp.concatenate([packed_key_rows, values], axis=1)
    attended, weight = exchange_attention(queries, kv, seg_q, seg_k, proj_weight, kv_heads)
    partial_rows = jnp.dot(attended, weight, preferred_element_type=jnp.float32)
    projected = sum_scatter(partial_rows.astype(jnp.bfloat16), moe_rows, 1)

    hidden_mid = (residual.astype(jnp.float32) + projected).astype(jnp.bfloat16)
    mid_float = lax.optimization_barrier(hidden_mid).astype(jnp.float32)
    inverse = lax.rsqrt(jnp.mean(mid_float * mid_float, axis=1, keepdims=True) + NORM_EPS)
    normed = (mid_float * inverse * norm_gain.astype(jnp.float32)[None, :]).astype(jnp.bfloat16)

    route_share = route_weights / jnp.sum(route_weights, axis=1, keepdims=True)
    named = expert_ids[:, :, None] == jnp.arange(experts, dtype=jnp.int32)[None, None, :]
    share = jnp.sum(jnp.where(named, route_share[:, :, None], 0.0), axis=1)
    share_high = lax.reduce_precision(share, 8, 7)
    share_low = (share - share_high).astype(jnp.bfloat16)
    pad = -(2 * experts) % 128
    sent = jnp.concatenate(
        [
            normed,
            share_high.astype(jnp.bfloat16),
            share_low,
            jnp.zeros((moe_rows, pad), jnp.bfloat16),
        ],
        axis=1,
    )
    gathered = gather_rows(sent, 2)
    expert = s * heads + c
    all_rows = gathered[:, :width]
    pair = gathered[:, width:].astype(jnp.float32)
    lane = jnp.arange(pair.shape[1], dtype=jnp.int32)[None, :]
    mine = jnp.logical_or(lane == expert, lane == expert + experts)
    own_share = jnp.sum(jnp.where(mine, pair, 0.0), axis=1, keepdims=True)
    gate_act = jnp.dot(all_rows, gate_weight[0], preferred_element_type=jnp.float32)
    up_act = jnp.dot(all_rows, up_weight[0], preferred_element_type=jnp.float32)
    hidden = (jax.nn.silu(gate_act) * up_act).astype(jnp.bfloat16)
    result = jnp.dot(hidden, down_weight[0], preferred_element_type=jnp.float32)
    mixed = (result * own_share).astype(jnp.bfloat16)
    mixture = sum_scatter(mixed, moe_rows, 3)
    return (hidden_mid, mixture.astype(jnp.bfloat16))


def solution(mesh):
    rows = P(("groups", "sect", "head"), None)
    split = P(("groups", "sect"), "head")
    expert = P(("sect", "head"), None, None)
    placed = (
        split,
        split,
        split,
        P("groups"),
        P("head", "sect"),
        rows,
        P(),
        rows,
        rows,
        expert,
        expert,
        expert,
    )
    return jax.shard_map(
        shards, mesh=mesh, in_specs=placed, out_specs=(rows, rows), check_vma=False
    )
```
